1024 devices in a mesh: ctx: 128 (over z, y_hi, core), dp: 8 (over x, y_lo).
Axes of the slice: x: 4, y: 8 (y_hi: 4, y_lo: 2; y = y_hi * 2 + y_lo), z: 16, core: 2. Of those that a mesh axis runs over, the one named last changes fastest.
Arguments:
- stream: bfloat16 [3, 16384, 8192], P(None, 'ctx', 'dp'), may hold values from -6 to 6
- short_taps: float32 [3, 3, 8192], replicated, may hold values from -3.5 to 3.5
- decay_rate: float32 [16, 512], P('dp'), may hold values from 1.2207031e-05 to 0.1
- residue: float32 [16, 512], P('dp'), may hold values from -0.4472136 to 0.4472136
Outputs:
- gated_output: bfloat16 [16384, 8192], P('ctx', 'dp')
The draws below stay inside these ranges and needn't reach their ends.
All inputs are finite; a program needn't handle non-finite values.
Results may differ from the reference program's by a relative error of at most 0.002.
Values may be sent and summed in bfloat16 or wider, within the bound.
No kernel may reach another device: no remote copies, remote signals or barrier semaphores. Data moves between devices by JAX's collectives and lax.ppermute only.
A program may use at most 128 MiB of HBM per device.

```python
import math
import jax
import jax.numpy as jnp
from jax import lax

D = 8192
GROUP = 16
ORDER = 16
TAPS = 3
G = 512
TOKENS = 16384


def filter_pair(key):
    base_key = jax.random.fold_in(key, 31)
    pick_key, rate_key, signs_key = jax.random.split(base_key, 3)
    slow_share = 0.5
    slow_pick = jax.random.bernoulli(pick_key, slow_share, (ORDER, G))
    unit_draw = jax.random.uniform(rate_key, (ORDER, G), jnp.float32)
    slow_rate = jnp.exp(jnp.log(0.2 / TOKENS) + unit_draw * jnp.log(10.0))
    fast_rate = jnp.exp(jnp.log(0.02) + unit_draw * jnp.log(5.0))
    rate_value = jnp.where(slow_pick, slow_rate, fast_rate)
    signs_draw = jnp.clip(jax.random.normal(signs_key, (ORDER, G), jnp.float32), -4.0, 4.0)
    return (rate_value, signs_draw * jnp.sqrt(2.0 * rate_value / ORDER))


def draw_decay_rate(key, part):
    return filter_pair(key)[0]


def draw_residue(key, part):
    return filter_pair(key)[1]


def levels(stream_key, shape, cuts, least, top_value):
    loudness = 1.0
    for dim, blocks in cuts:
        draws = jax.random.uniform(jax.random.fold_in(jax.random.fold_in(stream_key, 6), dim), (blocks,), jnp.float32, least / len(cuts), top_value / len(cuts))
        loudness = loudness * jnp.repeat(jnp.exp(draws), shape[dim] // blocks).reshape((-1,) + (1,) * (len(shape) - 1 - dim))
    return loudness


def scatter_about(key, dims, scale, bound, pieces=(), kind=jnp.bfloat16):
    values = scale * jax.random.normal(key, dims, jnp.float32)
    if pieces:
        values = values * levels(key, dims, pieces, -0.22, 0.18)
    return jnp.clip(values, -bound, bound).astype(kind)


def setup_inputs(seed: int = 0) -> dict:
    arg_keys = jax.random.split(jax.random.key(seed), 5)
    stream = scatter_about(arg_keys[0], (3, TOKENS, D), 1.0, 6.0, ((1, 128), (2, 8)))
    short_taps = scatter_about(arg_keys[1], (3, TAPS, D), TAPS ** -0.5, 3.5, (), jnp.float32)
    decay_rate = draw_decay_rate(jax.random.fold_in(arg_keys[4], 71), 0)
    residue = draw_residue(jax.random.fold_in(arg_keys[4], 71), 0)
    return {"stream": stream, "short_taps": short_taps, "decay_rate": decay_rate, "residue": residue}


def unfold_taps(seq_taps):
    group_count, length = seq_taps.shape
    padded = jnp.concatenate([seq_taps, jnp.zeros((group_count, length + 1), seq_taps.dtype)], 1)
    tiled = jnp.tile(padded, (1, length))[:, : 2 * length * length]
    return tiled.reshape(group_count, length, 2 * length)[:, :, :length]


def reference(stream, short_taps, decay_rate, residue):
    total = stream.shape[1]
    chan_count = stream.shape[2]
    group_count = chan_count // GROUP
    reach = short_taps.shape[1] - 1
    widened = jnp.pad(stream.astype(jnp.float32), ((0, 0), (reach, 0), (0, 0)))
    features = short_taps[:, 0, None, :] * widened[:, reach:, :]
    for lag in range(1, reach + 1):
        features = features + short_taps[:, lag, None, :] * widened[:, reach - lag: reach - lag + total, :]
    query = features[0]
    product = features[1] * features[2]
    block = math.gcd(total, 128)
    position = jnp.arange(block, dtype=jnp.float32)
    powers = jnp.exp(-decay_rate[:, :, None] * position)
    seq_taps = jnp.sum(residue[:, :, None] * powers, 0)
    toeplitz = unfold_taps(seq_taps)
    closing = jnp.exp(-decay_rate[:, :, None] * (block - 1.0 - position))
    opening = residue[:, :, None] * jnp.exp(-decay_rate[:, :, None] * (position + 1.0))
    span_decay = jnp.exp(-decay_rate * block)
    blocks = product.reshape(total // block, block, group_count, GROUP)

    def advance(state, piece):
        local_part = jnp.einsum('gst,sgc->tgc', toeplitz, piece, precision=lax.Precision.HIGHEST)
        tail_part = jnp.einsum('rgt,rgc->tgc', opening, state, precision=lax.Precision.HIGHEST)
        fresh = jnp.einsum('rgs,sgc->rgc', closing, piece, precision=lax.Precision.HIGHEST)
        return span_decay[:, :, None] * state + fresh, local_part + tail_part

    start_state = jnp.zeros((ORDER, group_count, GROUP), jnp.float32)
    final_state, convolved = lax.scan(advance, start_state, blocks)
    convolved = convolved.reshape(total, chan_count)
    return (query * convolved).astype(jnp.bfloat16)
```

```python
import functools

import jax
import jax.numpy as jnp
from jax import lax
from jax.experimental import pallas as pl
from jax.experimental.pallas import tpu as pltpu
from jax.sharding import PartitionSpec as P


GROUP = 16
ORDER = 16
TAPS = 3
CUTS = 2
RUNS = 8
JUMPS = (1, 4, 3, 2)
LANES = 128
SUB = 8
F32 = jnp.float32


def low_half(shape):
    return lax.broadcasted_iota(jnp.int32, shape, len(shape) - 1) < LANES // 2


def pick(mask, low, high):
    return jnp.where(mask, low, high)


def half_turn(x):
    return pltpu.roll(x, LANES // 2, x.ndim - 1)


def swap_parts(vectors):
    width = LANES // CUTS
    part = lax.broadcasted_iota(jnp.int32, vectors[0].shape, 1) // width
    results = []
    for c in range(CUTS):
        result = vectors[c]
        for b in range(CUTS):
            if b != c:
                result = jnp.where(part == b, pltpu.roll(vectors[b], (b - c) % CUTS * width, 1), result)
        results.append(result)
    return results


def store_slices(ref, vectors):
    rows = ORDER // CUTS
    for a in range(rows):
        for c, vector in enumerate(swap_parts([vectors[a + rows * b] for b in range(CUTS)])):
            ref[pl.ds(rows * c + a, SUB, stride=ORDER), :] = vector


def load_slices(ref):
    rows = ORDER // CUTS
    vectors = [None] * ORDER
    for a in range(rows):
        parts = [ref[pl.ds(rows * c + a, SUB, stride=ORDER), :] for c in range(CUTS)]
        for b, vector in enumerate(swap_parts(parts)):
            vectors[a + rows * b] = vector
    return vectors


def pack_kernel(stream, taps, rates, residues, tail_ref, out_ref, taps_ref, rows_v, taps_v, rate_v, residue_v, sems):
    count, rows, chans = stream.shape
    held = rows_v.shape[1]
    offset = pl.multiple_of(lax.axis_index("dp") * chans, LANES)
    copies = [
        pltpu.make_async_copy(rates, rate_v, sems.at[0]),
        pltpu.make_async_copy(residues, residue_v, sems.at[1]),
        pltpu.make_async_copy(stream.at[:, pl.ds(rows - held, held), :], rows_v, sems.at[2]),
        pltpu.make_async_copy(taps.at[:, :, pl.ds(offset, chans)], taps_v, sems.at[3]),
    ]
    for copy in copies:
        copy.start()
    copies[0].wait()
    copies[1].wait()
    mask = low_half((rate_v.shape[0], LANES))
    for q in range(rate_v.shape[1] // LANES):
        rate = rate_v[:, q * LANES : (q + 1) * LANES]
        residue = residue_v[:, q * LANES : (q + 1) * LANES]
        out_ref[2 * q] = pick(mask, rate, half_turn(residue))
        out_ref[2 * q + 1] = pick(mask, half_turn(rate), residue)
    copies[2].wait()
    tail_ref[...] = rows_v[:, held - tail_ref.shape[1] :, :]
    copies[3].wait()
    blocks = chans // LANES
    for i in range(count):
        for lag in range(TAPS):
            for j in range(blocks):
                taps_ref[pl.ds((i * TAPS + lag) * blocks + j, 1), :] = taps_v[
                    i, pl.ds(lag, 1), j * LANES : (j + 1) * LANES
                ]


def features_kernel(stream_ref, halo_ref, taps_ref, product_ref, query_ref, wide_ref):
    rows = stream_ref.shape[1]
    blocks = stream_ref.shape[2] // LANES
    span = SUB * blocks
    for i in range(3):
        for j in range(blocks):
            cols = slice(j * LANES, (j + 1) * LANES)
            wide_ref[i, pl.ds(j * SUB + SUB - TAPS + 1, TAPS - 1), :] = halo_ref[i, :, cols].astype(F32)
            for pair in range(rows // (2 * SUB)):
                both = stream_ref[i, pair * 2 * SUB : (pair + 1) * 2 * SUB, cols].astype(F32)
                base = (2 * pair + 1) * span + j * SUB
                wide_ref[i, pl.ds(base, SUB), :] = both[:SUB]
                wide_ref[i, pl.ds(base + span, SUB), :] = both[SUB:]
    taps = [[taps_ref[pl.ds((i * TAPS + lag) * blocks, blocks), :] for lag in range(TAPS)] for i in range(3)]

    def token(i, start, s):
        return wide_ref[i, pl.ds(start + s, blocks, stride=SUB), :]

    def step(b, carry):
        before = [list(c) for c in carry]
        start = pl.multiple_of((b + 1) * span, span)
        for s in range(SUB):
            feats = []
            for i in range(3):
                now = token(i, start, s)
                older, old = before[i]
                feats.append(taps[i][0] * now + taps[i][1] * old + taps[i][2] * older)
                before[i] = [old, now]
            at = pl.multiple_of(b * span + s * blocks, blocks)
            query_ref[pl.ds(at, blocks), :] = feats[0]
            product_ref[pl.ds(at, blocks), :] = feats[1] * feats[2]
        return tuple(tuple(c) for c in before)

    first = tuple((token(i, 0, SUB - 2), token(i, 0, SUB - 1)) for i in range(3))
    lax.fori_loop(0, rows // SUB, step, first)


def state_kernel(product_ref, poles_ref, state_ref, decay_ref, residue_ref, rate_ref, wide_ref):
    blocks = SUB
    rows = product_ref.shape[0] // blocks
    poles = poles_ref[...]
    lane = lax.broadcasted_iota(jnp.int32, (ORDER, LANES), 1)
    for j in range(blocks):
        group = lane // GROUP + j * (LANES // GROUP)
        wide_ref[0, pl.ds(j * ORDER, ORDER), :] = jnp.take_along_axis(poles, group, axis=1)
        wide_ref[1, pl.ds(j * ORDER, ORDER), :] = jnp.take_along_axis(poles, group + LANES // 2, axis=1)
    rates, decays = [], []
    for r in range(ORDER):
        rate = wide_ref[0, pl.ds(r, blocks, stride=ORDER), :]
        decay = jnp.exp(-rate)
        decay_ref[pl.ds(r * blocks, blocks), :] = decay
        residue_ref[pl.ds(r * blocks, blocks), :] = wide_ref[1, pl.ds(r, blocks, stride=ORDER), :]
        rates.append(rate)
        decays.append(decay)
    store_slices(rate_ref, rates)

    def step(b, states):
        states = list(states)
        for s in range(SUB):
            p = product_ref[pl.ds(pl.multiple_of((b * SUB + s) * blocks, blocks), blocks), :]
            states = [decays[r] * states[r] + p for r in range(ORDER)]
        return tuple(states)

    zero = jnp.zeros((blocks, LANES), F32)
    store_slices(state_ref, lax.fori_loop(0, rows // SUB, step, (zero,) * ORDER))


def near_kernel(span, parts_ref, rate_ref, total_ref, decay_ref, far_ref, prefix_ref):
    count = parts_ref.shape[0]
    rate = rate_ref[lax.rem(lax.axis_index("ctx"), count)]
    decay = jnp.exp(-rate * float(span))
    decay_ref[...] = decay
    far_ref[...] = jnp.exp(-rate * float(span * count))
    run = jnp.zeros(rate.shape, F32)
    for k in range(count):
        prefix_ref[k] = run
        run = decay * run + parts_ref[k]
    total_ref[...] = run


def spread_kernel(run_ref, decay_ref, prefix_ref, out_ref):
    run = run_ref[...]
    for k in range(out_ref.shape[0]):
        out_ref[k] = prefix_ref[k] + run
        run = decay_ref[...] * run


def output_kernel(state_ref, product_ref, query_ref, decay_ref, residue_ref, out_ref, wide_ref):
    blocks = SUB
    span = SUB * blocks
    rows = product_ref.shape[0] // blocks
    decays = [decay_ref[pl.ds(r * blocks, blocks), :] for r in range(ORDER)]
    residues = [residue_ref[pl.ds(r * blocks, blocks), :] for r in range(ORDER)]

    def step(b, states):
        states = list(states)
        for s in range(SUB):
            at = pl.multiple_of((b * SUB + s) * blocks, blocks)
            p = product_ref[pl.ds(at, blocks), :]
            states = [decays[r] * states[r] + p for r in range(ORDER)]
            terms = [residues[r] * states[r] for r in range(ORDER)]
            while len(terms) > 1:
                terms = [terms[k] + terms[k + 1] for k in range(0, len(terms), 2)]
            wide_ref[pl.ds(b * span + s, blocks, stride=SUB), :] = query_ref[pl.ds(at, blocks), :] * terms[0]
        return tuple(states)

    lax.fori_loop(0, rows // SUB, step, tuple(load_slices(state_ref)))
    for pair in range(rows // (2 * SUB)):
        for j in range(blocks):
            base = 2 * pair * span + j * SUB
            both = jnp.concatenate([wide_ref[pl.ds(base, SUB), :], wide_ref[pl.ds(base + span, SUB), :]], 0)
            out_ref[pair * 2 * SUB : (pair + 1) * 2 * SUB, j * LANES : (j + 1) * LANES] = both.astype(jnp.bfloat16)


def shape(*dims):
    return pltpu.VMEM(dims, F32)


def call(kernel, out_shape, inputs, scratch=()):
    return pl.pallas_call(kernel, out_shape=out_shape, scratch_shapes=list(scratch))(
        *[pltpu.with_memory_space_constraint(x, pltpu.VMEM) for x in inputs]
    )


def exchange(x, groups):
    return lax.all_to_all(x, "ctx", split_axis=0, concat_axis=0, tiled=True, axis_index_groups=groups)


def earlier_runs(total, decay, run):
    def send(value, routes):
        pairs = [(a * run + k, b * run + k) for a, b in routes for k in range(run)]
        return lax.ppermute(value, "ctx", pairs)

    half = RUNS // 2
    before = None
    upto = total
    for z in range(half - 1):
        got = send(upto, [(z, z + 1)])
        before = got if before is None else before + got
        upto = decay * before + total
    got = {far: send(upto, [(z, z + far) for z in range(half - 1, RUNS - far)]) for far in JUMPS}
    later = got[half]
    for far in range(half - 1, 0, -1):
        later = decay * later + got[far]
    return before + later


def block(stream, short_taps, decay_rate, residue):
    rows, chans = stream.shape[1], stream.shape[2]
    blocks = chans // LANES
    ctx_size, dp_size = lax.axis_size("ctx"), lax.axis_size("dp")
    reach = TAPS - 1

    anywhere = pl.BlockSpec(memory_space=pl.ANY)
    tail, packed, taps = pl.pallas_call(
        pack_kernel,
        in_specs=[anywhere] * 4,
        out_shape=(
            pltpu.VMEM((3, reach, chans), stream.dtype),
            shape(dp_size, decay_rate.shape[0], LANES),
            shape(3 * TAPS * blocks, LANES),
        ),
        scratch_shapes=[
            pltpu.VMEM((3, 2 * SUB, chans), stream.dtype),
            pltpu.VMEM((3, TAPS, chans), F32),
            pltpu.VMEM(decay_rate.shape, F32),
            pltpu.VMEM(residue.shape, F32),
            pltpu.SemaphoreType.DMA((4,)),
        ],
        name="pack",
    )(stream, short_taps, decay_rate, residue)
    halo = lax.ppermute(tail, "ctx", [(k, k + 1) for k in range(ctx_size - 1)])
    poles = lax.all_to_all(packed, "dp", split_axis=0, concat_axis=0, tiled=True)
    poles = poles.reshape(ORDER, LANES)

    token_major = shape(rows * blocks, LANES)
    product, query = call(
        features_kernel,
        (token_major, token_major),
        (stream, halo, taps),
        (pltpu.VMEM((3, (rows // SUB + 1) * SUB * blocks, LANES), F32),),
    )
    table = shape(ORDER * blocks, LANES)
    state, decay, gain, rate = call(
        state_kernel, (table, table, table, table), (product, poles), (pltpu.VMEM((2, ORDER * blocks, LANES), F32),)
    )

    run = ctx_size // RUNS
    part = ORDER // CUTS
    near = [[z * run + k for k in range(run)] for z in range(RUNS)]
    parts = exchange(state.reshape(run, part, LANES), near)
    piece = shape(part, LANES)
    total, decay_near, decay_far, prefix = call(
        functools.partial(near_kernel, rows),
        (piece, piece, piece, shape(run, part, LANES)),
        (parts, rate.reshape(run, part, LANES)),
    )
    before = earlier_runs(total, decay_far, run)
    starts = call(spread_kernel, shape(run, part, LANES), (before, decay_near, prefix))
    start = exchange(starts, near)
    return call(
        output_kernel,
        jax.ShapeDtypeStruct((rows, chans), jnp.bfloat16),
        (start.reshape(ORDER * blocks, LANES), product, query, decay, gain),
        (pltpu.VMEM((rows * blocks, LANES), F32),),
    )


def solution(mesh):
    in_specs = (P(None, "ctx", "dp"), P(), P("dp", None), P("dp", None))
    out_specs = P("ctx", "dp")
    return jax.shard_map(block, mesh=mesh, in_specs=in_specs, out_specs=out_specs, check_vma=False)
```

```python
import functools

import jax
import jax.numpy as jnp
from jax import lax
from jax.experimental import pallas as pl
from jax.experimental.pallas import tpu as pltpu
from jax.sharding import PartitionSpec as P


GROUP = 16
ORDER = 16
TAPS = 3
LANES = 128
SUB = 8
CUTS = 2
PART = ORDER // CUTS
EDGES = 5
SEND = PART + EDGES
BACK = PART + 3
RUNS = 8
CHAIN = 5
JUMPS = (3, 2, 1)
F32 = jnp.float32


def low_half(shape):
    return lax.broadcasted_iota(jnp.int32, shape, len(shape) - 1) < LANES // 2


def half_turn(x):
    return pltpu.roll(x, LANES // 2, x.ndim - 1)


def swap_halves(first, second):
    mask = low_half(first.shape)
    return jnp.where(mask, first, half_turn(second)), jnp.where(mask, half_turn(first), second)


def store_slices(ref, vectors, chunk):
    for a in range(PART):
        for c, vector in enumerate(swap_halves(vectors[a], vectors[a + PART])):
            ref[pl.ds(chunk * c + a, SUB, stride=CUTS * chunk), :] = vector


def load_pair(ref, row):
    return swap_halves(*[ref[pl.ds(BACK * c + row, SUB, stride=CUTS * BACK), :] for c in range(CUTS)])


def pack_kernel(stream, taps, rates, residues, out_ref, stream_ref, taps_ref, taps_v, rate_v, residue_v, sems):
    count, _, chans = taps_v.shape
    offset = pl.multiple_of(lax.axis_index("dp") * chans, LANES)
    copies = [
        pltpu.make_async_copy(rates, rate_v, sems.at[0]),
        pltpu.make_async_copy(residues, residue_v, sems.at[1]),
        pltpu.make_async_copy(taps.at[:, :, pl.ds(offset, chans)], taps_v, sems.at[2]),
        pltpu.make_async_copy(stream, stream_ref, sems.at[3]),
    ]
    for copy in copies:
        copy.start()
    copies[0].wait()
    copies[1].wait()
    mask = low_half((rate_v.shape[0], LANES))
    for q in range(rate_v.shape[1] // LANES):
        rate = rate_v[:, q * LANES : (q + 1) * LANES]
        residue = residue_v[:, q * LANES : (q + 1) * LANES]
        out_ref[2 * q] = jnp.where(mask, rate, half_turn(residue))
        out_ref[2 * q + 1] = jnp.where(mask, half_turn(rate), residue)
    copies[2].wait()
    blocks = chans // LANES
    for i in range(count):
        for lag in range(TAPS):
            for j in range(blocks):
                taps_ref[pl.ds((i * TAPS + lag) * blocks + j, 1), :] = taps_v[
                    i, pl.ds(lag, 1), j * LANES : (j + 1) * LANES
                ]
    copies[3].wait()


def spread_tokens(source_ref, wide_ref, pairs):
    blocks = source_ref.shape[1] // LANES
    span = SUB * blocks
    for pair in pairs:
        for j in range(blocks):
            both = source_ref[pair * 2 * SUB : (pair + 1) * 2 * SUB, j * LANES : (j + 1) * LANES].astype(F32)
            base = 2 * pair * span + j * SUB
            wide_ref[pl.ds(base, SUB), :] = both[:SUB]
            wide_ref[pl.ds(base + span, SUB), :] = both[SUB:]


def load_taps(taps_ref, blocks, i):
    return [taps_ref[pl.ds((i * TAPS + lag) * blocks, blocks), :] for lag in range(TAPS)]


def features_kernel(stream_ref, taps_ref, after_ref, product_ref, edge_ref, wide_ref):
    rows = stream_ref.shape[1]
    blocks = stream_ref.shape[2] // LANES
    span = SUB * blocks
    last_pair = rows // (2 * SUB) - 1
    for i in range(3):
        spread_tokens(stream_ref.at[i], wide_ref.at[i], range(last_pair + 1) if i else (last_pair,))
    taps = [load_taps(taps_ref, blocks, i) for i in range(3)]

    def token(i, start, s):
        return wide_ref[i, pl.ds(start + s, blocks, stride=SUB), :]

    def step(b, carry):
        before = [list(c) for c in carry]
        start = pl.multiple_of(b * span, span)
        for s in range(SUB):
            feats = []
            for i in (1, 2):
                now = token(i, start, s)
                older, old = before[i - 1]
                feats.append(taps[i][0] * now + taps[i][1] * old + taps[i][2] * older)
                before[i - 1] = [old, now]
            product_ref[pl.ds(pl.multiple_of(b * span + s * blocks, blocks), blocks), :] = feats[0] * feats[1]
        return tuple(tuple(c) for c in before)

    zero = jnp.zeros((blocks, LANES), F32)
    lax.fori_loop(0, rows // SUB, step, ((zero, zero),) * 2)

    def put(row, value):
        edge_ref[pl.ds(row * blocks, blocks), :] = value

    for i in range(3):
        old, now = token(i, (rows - SUB) * blocks, SUB - 2), token(i, (rows - SUB) * blocks, SUB - 1)
        put(2 * i, taps[i][1] * now + taps[i][2] * old)
        put(2 * i + 1, taps[i][2] * now)
    for i in (1, 2):
        first, second = token(i, 0, 0), token(i, 0, 1)
        put(2 * i + 4, taps[i][0] * first)
        put(2 * i + 5, taps[i][0] * second + taps[i][1] * first)
    product_ref[pl.ds(0, blocks), :] = zero
    product_ref[pl.ds(blocks, blocks), :] = zero


def state_kernel(product_ref, poles_ref, edge_ref, state_ref, decay_ref, residue_ref, rate_ref, wide_ref):
    blocks = SUB
    rows = product_ref.shape[0] // blocks
    poles = poles_ref[...]
    lane = lax.broadcasted_iota(jnp.int32, (ORDER, LANES), 1)
    for j in range(blocks):
        group = lane // GROUP + j * (LANES // GROUP)
        wide_ref[0, pl.ds(j * ORDER, ORDER), :] = jnp.take_along_axis(poles, group, axis=1)
        wide_ref[1, pl.ds(j * ORDER, ORDER), :] = jnp.take_along_axis(poles, group + LANES // 2, axis=1)
    rates, decays = [], []
    for r in range(ORDER):
        rate = wide_ref[0, pl.ds(r, blocks, stride=ORDER), :]
        decay = jnp.exp(-rate)
        decay_ref[pl.ds(r * blocks, blocks), :] = decay
        residue_ref[pl.ds(r * blocks, blocks), :] = wide_ref[1, pl.ds(r, blocks, stride=ORDER), :]
        rates.append(rate)
        decays.append(decay)
    store_slices(rate_ref, rates, PART)
    for n in range(EDGES):
        parts = swap_halves(*[edge_ref[pl.ds((2 * n + t) * blocks, blocks), :] for t in range(2)])
        for c in range(CUTS):
            state_ref[pl.ds(SEND * c + PART + n, SUB, stride=CUTS * SEND), :] = parts[c]
    zero = jnp.zeros((blocks, LANES), F32)

    def step(b, states):
        states = list(states)
        for s in range(SUB):
            p = product_ref[pl.ds(pl.multiple_of((b * SUB + s) * blocks, blocks), blocks), :]
            states = [decays[r] * states[r] + p for r in range(ORDER)]
        return tuple(states)

    store_slices(state_ref, lax.fori_loop(0, rows // SUB, step, (zero,) * ORDER), SEND)


def local_kernel(product_ref, decay_ref, residue_ref, taps_ref, after_ref, stream, out_ref, query_ref, source_v, wide_ref, sem):
    blocks = SUB
    span = SUB * blocks
    rows = product_ref.shape[0] // blocks
    copy = pltpu.make_async_copy(stream.at[0], source_v, sem.at[0])
    copy.start()
    decays = [decay_ref[pl.ds(r * blocks, blocks), :] for r in range(ORDER)]
    residues = [residue_ref[pl.ds(r * blocks, blocks), :] for r in range(ORDER)]

    def step(b, states):
        states = list(states)
        for s in range(SUB):
            at = pl.ds(pl.multiple_of((b * SUB + s) * blocks, blocks), blocks)
            p = product_ref[at, :]
            states = [decays[r] * states[r] + p for r in range(ORDER)]
            out_ref[at, :] = total([residues[r] * states[r] for r in range(ORDER)])
        return tuple(states)

    zero = jnp.zeros((blocks, LANES), F32)
    lax.fori_loop(0, rows // SUB, step, (zero,) * ORDER)
    copy.wait()
    spread_tokens(source_v, wide_ref, range(rows // (2 * SUB)))
    taps = load_taps(taps_ref, blocks, 0)

    def filtered(b, before):
        older, old = before
        for s in range(SUB):
            now = wide_ref[pl.ds(pl.multiple_of(b * span, span) + s, blocks, stride=SUB), :]
            at = pl.ds(pl.multiple_of((b * SUB + s) * blocks, blocks), blocks)
            query_ref[at, :] = taps[0] * now + taps[1] * old + taps[2] * older
            older, old = old, now
        return older, old

    lax.fori_loop(0, rows // SUB, filtered, (zero, zero))


def total(terms):
    while len(terms) > 1:
        terms = [terms[k] + terms[k + 1] for k in range(0, len(terms), 2)]
    return terms[0]


def edge_state(own, previous, powers_ref):
    product = (own[3:4] + previous[1:2]) * (own[4:5] + previous[2:3])
    mask = low_half(product.shape)
    turned = half_turn(product)
    return powers_ref[0] * jnp.where(mask, product, turned) + powers_ref[1] * jnp.where(mask, turned, product)


def near_kernel(rows, parts_ref, rate_ref, message_ref, powers_ref, prefix_ref, halo_ref):
    count = parts_ref.shape[0] // SEND
    position = lax.axis_index("ctx")
    rate = rate_ref[lax.rem(position, count)]
    for n, length in enumerate((rows - 1, rows - 2, rows, rows * (count - 1), rows * count)):
        powers_ref[n] = jnp.exp(-rate * float(length))
    run = jnp.zeros(rate.shape, F32)
    none = jnp.zeros((3, LANES), F32)
    previous = none
    halo_ref[:3, :] = none
    for k in range(count):
        prefix_ref[k] = run
        new = parts_ref[pl.ds(SEND * k, PART), :]
        edges = parts_ref[pl.ds(SEND * k + PART, EDGES), :]
        if k:
            halo_ref[pl.ds(3 * k, 3), :] = previous
            new = new + edge_state(edges, previous, powers_ref)
        run = powers_ref[2] * run + new
        previous = edges[:3]
    first = parts_ref[pl.ds(PART, EDGES), :]
    start = run + powers_ref[3] * edge_state(first, none, powers_ref)
    message_ref[:PART, :] = jnp.where(position < count, start, run)
    message_ref[pl.ds(PART, 3), :] = previous
    message_ref[pl.ds(PART + 3, 2), :] = first[3:]


def link_kernel(z, count, message_ref, heard_ref, got_ref, powers_ref, message_out, heard_out):
    heard_out[...] = heard_ref[...] + got_ref[...]
    mine = message_ref[:PART, :]
    edges = message_ref[pl.ds(PART, EDGES), :]
    whole = powers_ref[4] * got_ref[:PART, :] + mine
    whole = whole + powers_ref[3] * edge_state(edges, got_ref[pl.ds(PART, EDGES), :], powers_ref)
    message_out[:PART, :] = jnp.where(lax.axis_index("ctx") // count == z + 1, whole, mine)
    message_out[pl.ds(PART, EDGES), :] = edges


def spread_kernel(message_ref, heard_ref, jumps_ref, powers_ref, prefix_ref, halo_ref, out_ref):
    count = prefix_ref.shape[0]
    index = lax.axis_index("ctx") // count
    run = heard_ref[:PART, :]
    halo = heard_ref[pl.ds(PART, EDGES), :]
    for n, far in enumerate(JUMPS):
        source = index - far
        value = jumps_ref[n][:PART, :]
        edges = jumps_ref[n][pl.ds(PART, EDGES), :]
        later = powers_ref[4] * run + value + powers_ref[3] * edge_state(edges, halo, powers_ref)
        run = jnp.where(source == CHAIN - 1, value, jnp.where(source >= CHAIN, later, run))
        halo = jnp.where(source >= CHAIN - 1, edges, halo)
    first = edge_state(message_ref[pl.ds(PART, EDGES), :], halo, powers_ref)
    for k in range(count):
        out_ref[pl.ds(BACK * k, PART), :] = prefix_ref[k] + run
        out_ref[pl.ds(BACK * k + PART, 3), :] = halo_ref[pl.ds(3 * k, 3), :] if k else halo[:3]
        run = powers_ref[2] * run
        if k == 0:
            run = run + first


def output_kernel(start_ref, product_ref, query_ref, edge_ref, local_ref, decay_ref, residue_ref, out_ref, wide_ref):
    blocks = SUB
    span = SUB * blocks
    rows = product_ref.shape[0] // blocks
    decays = [decay_ref[pl.ds(r * blocks, blocks), :] for r in range(ORDER)]
    residues = [residue_ref[pl.ds(r * blocks, blocks), :] for r in range(ORDER)]
    pairs = [load_pair(start_ref, a) for a in range(PART)]
    states = [low for low, _ in pairs] + [high for _, high in pairs]

    halos = [load_pair(start_ref, PART + n) for n in range(3)]
    carried = states
    for s in range(TAPS - 1):
        one, two = [edge_ref[pl.ds((2 * n + s) * blocks, blocks), :] + halos[n - 2][s] for n in (3, 4)]
        carried = [decays[r] * carried[r] + one * two for r in range(ORDER)]
        terms = [residues[r] * carried[r] for r in range(ORDER)]
        q = query_ref[pl.ds(s * blocks, blocks), :] + halos[0][s]
        wide_ref[pl.ds(s, blocks, stride=SUB), :] = q * total(terms)

    def token(b, s, terms):
        at = pl.ds(pl.multiple_of((b * SUB + s) * blocks, blocks), blocks)
        terms = [decays[r] * terms[r] for r in range(ORDER)]
        wide_ref[pl.ds(b * span + s, blocks, stride=SUB), :] = query_ref[at, :] * (local_ref[at, :] + total(terms))
        return terms

    def step(b, terms):
        terms = list(terms)
        for s in range(SUB):
            terms = token(b, s, terms)
        return tuple(terms)

    for s in range(TAPS - 1, SUB):
        terms = token(0, s, terms)
    lax.fori_loop(1, rows // SUB, step, tuple(terms))
    for pair in range(rows // (2 * SUB)):
        for j in range(blocks):
            base = 2 * pair * span + j * SUB
            both = jnp.concatenate([wide_ref[pl.ds(base, SUB), :], wide_ref[pl.ds(base + span, SUB), :]], 0)
            out_ref[pair * 2 * SUB : (pair + 1) * 2 * SUB, j * LANES : (j + 1) * LANES] = both.astype(jnp.bfloat16)


def shape(*dims):
    return pltpu.VMEM(dims, F32)


def call(kernel, out_shape, inputs, scratch=()):
    return pl.pallas_call(kernel, out_shape=out_shape, scratch_shapes=list(scratch))(
        *[pltpu.with_memory_space_constraint(x, pltpu.VMEM) for x in inputs]
    )


def exchange(x, groups):
    flat = x.reshape(len(groups[0]), 1, -1)
    flat = lax.all_to_all(flat, "ctx", split_axis=0, concat_axis=0, tiled=True, axis_index_groups=groups)
    return flat.reshape(x.shape)


def earlier_runs(message, powers, run):
    def send(value, routes):
        pairs = [(a * run + k, b * run + k) for a, b in routes for k in range(run)]
        return lax.ppermute(value, "ctx", pairs)

    heard = jnp.zeros((SEND, LANES), F32)
    row = shape(SEND, LANES)
    for z in range(CHAIN - 1):
        got = send(message, [(z, z + 1)])
        message, heard = call(functools.partial(link_kernel, z, run), (row, row), (message, heard, got, powers))
    jumps = [send(message, [(z, z + far) for z in range(CHAIN - 1, RUNS - far)]) for far in JUMPS]
    return message, heard, jumps


def block(stream, short_taps, decay_rate, residue):
    rows, chans = stream.shape[1], stream.shape[2]
    blocks = chans // LANES
    ctx_size, dp_size = lax.axis_size("ctx"), lax.axis_size("dp")

    packed, near_stream, taps = pl.pallas_call(
        pack_kernel,
        in_specs=[pl.BlockSpec(memory_space=pl.ANY)] * 4,
        out_shape=(
            shape(dp_size, decay_rate.shape[0], LANES),
            pltpu.VMEM(stream.shape, stream.dtype),
            shape(3 * TAPS * blocks, LANES),
        ),
        scratch_shapes=[
            pltpu.VMEM((3, TAPS, chans), F32),
            pltpu.VMEM(decay_rate.shape, F32),
            pltpu.VMEM(residue.shape, F32),
            pltpu.SemaphoreType.DMA((4,)),
        ],
        name="pack",
    )(stream, short_taps, decay_rate, residue)
    poles = lax.all_to_all(packed, "dp", split_axis=0, concat_axis=0, tiled=True)
    poles = poles.reshape(ORDER, LANES)

    token_major = shape(rows * blocks, LANES)
    product, edges = call(
        features_kernel,
        (token_major, shape(2 * EDGES * blocks, LANES)),
        (near_stream, taps, poles),
        (pltpu.VMEM((3, rows * blocks, LANES), F32),),
    )
    table = shape(ORDER * blocks, LANES)
    run = ctx_size // RUNS
    state, decay, gain, rate = call(
        state_kernel,
        (shape(run * SEND, LANES), table, table, table),
        (product, poles, edges),
        (pltpu.VMEM((2, ORDER * blocks, LANES), F32),),
    )

    near = [[z * run + k for k in range(run)] for z in range(RUNS)]
    parts = exchange(state, near)
    message, powers, prefix, halos = call(
        functools.partial(near_kernel, rows),
        (shape(SEND, LANES), shape(5, PART, LANES), shape(run, PART, LANES), shape(3 * run, LANES)),
        (parts, rate.reshape(run, PART, LANES)),
    )
    vmem = functools.partial(pltpu.with_memory_space_constraint, memory_space=pltpu.VMEM)
    local, query = pl.pallas_call(
        local_kernel,
        in_specs=[pl.BlockSpec(memory_space=pltpu.VMEM)] * 5 + [pl.BlockSpec(memory_space=pl.ANY)],
        out_shape=(token_major, token_major),
        scratch_shapes=[
            pltpu.VMEM((rows, chans), stream.dtype),
            pltpu.VMEM((rows * blocks, LANES), F32),
            pltpu.SemaphoreType.DMA((1,)),
        ],
        name="local",
    )(vmem(product), vmem(decay), vmem(gain), vmem(taps), vmem(message), stream)
    message, heard, jumps = earlier_runs(message, powers, run)

    def spread(message_ref, heard_ref, *refs):
        spread_kernel(message_ref, heard_ref, refs[: len(jumps)], *refs[len(jumps) :])

    starts = call(spread, shape(run * BACK, LANES), (message, heard, *jumps, powers, prefix, halos))
    return call(
        output_kernel,
        jax.ShapeDtypeStruct((rows, chans), jnp.bfloat16),
        (exchange(starts, near), product, query, edges, local, decay, gain),
        (pltpu.VMEM((rows * blocks, LANES), F32),),
    )


def solution(mesh):
    in_specs = (P(None, "ctx", "dp"), P(), P("dp", None), P("dp", None))
    out_specs = P("ctx", "dp")
    return jax.shard_map(block, mesh=mesh, in_specs=in_specs, out_specs=out_specs, check_vma=False)
```

```python
import functools

import jax
import jax.numpy as jnp
from jax import lax
from jax.experimental import pallas as pl
from jax.experimental.pallas import tpu as pltpu
from jax.sharding import PartitionSpec as P


GROUP = 16
ORDER = 16
TAPS = 3
LANES = 128
SUB = 8
CUTS = 2
PART = ORDER // CUTS
EDGES = 5
SEND = PART + EDGES
BACK = PART + 3
RUNS = 8
CHAIN = 5
JUMPS = (3, 2, 1)
PIECES = 4
F32 = jnp.float32


def low_half(shape):
    return lax.broadcasted_iota(jnp.int32, shape, len(shape) - 1) < LANES // 2


def half_turn(x):
    return pltpu.roll(x, LANES // 2, x.ndim - 1)


def swap_halves(first, second):
    mask = low_half(first.shape)
    return jnp.where(mask, first, half_turn(second)), jnp.where(mask, half_turn(first), second)


def store_slices(ref, vectors, chunk):
    for a in range(PART):
        for c, vector in enumerate(swap_halves(vectors[a], vectors[a + PART])):
            ref[pl.ds(chunk * c + a, SUB, stride=CUTS * chunk), :] = vector


def load_pair(ref, row):
    return swap_halves(*[ref[pl.ds(BACK * c + row, SUB, stride=CUTS * BACK), :] for c in range(CUTS)])


def pack_kernel(stream, taps, rates, residues, out_ref, stream_ref, taps_ref, taps_v, rate_v, residue_v, sems):
    count, _, chans = taps_v.shape
    offset = pl.multiple_of(lax.axis_index("dp") * chans, LANES)
    copies = [
        pltpu.make_async_copy(rates, rate_v, sems.at[0]),
        pltpu.make_async_copy(residues, residue_v, sems.at[1]),
        pltpu.make_async_copy(taps.at[:, :, pl.ds(offset, chans)], taps_v, sems.at[2]),
        pltpu.make_async_copy(stream, stream_ref, sems.at[3]),
    ]
    for copy in copies:
        copy.start()
    copies[0].wait()
    copies[1].wait()
    mask = low_half((rate_v.shape[0], LANES))
    for q in range(rate_v.shape[1] // LANES):
        rate = rate_v[:, q * LANES : (q + 1) * LANES]
        residue = residue_v[:, q * LANES : (q + 1) * LANES]
        out_ref[2 * q] = jnp.where(mask, rate, half_turn(residue))
        out_ref[2 * q + 1] = jnp.where(mask, half_turn(rate), residue)
    copies[2].wait()
    blocks = chans // LANES
    for i in range(count):
        for lag in range(TAPS):
            for j in range(blocks):
                taps_ref[pl.ds((i * TAPS + lag) * blocks + j, 1), :] = taps_v[
                    i, pl.ds(lag, 1), j * LANES : (j + 1) * LANES
                ]
    copies[3].wait()


def spread_tokens(source_ref, wide_ref, pairs):
    blocks = source_ref.shape[1] // LANES
    span = SUB * blocks
    for pair in pairs:
        for j in range(blocks):
            both = source_ref[pair * 2 * SUB : (pair + 1) * 2 * SUB, j * LANES : (j + 1) * LANES].astype(F32)
            base = 2 * pair * span + j * SUB
            wide_ref[pl.ds(base, SUB), :] = both[:SUB]
            wide_ref[pl.ds(base + span, SUB), :] = both[SUB:]


def load_taps(taps_ref, blocks, i):
    return [taps_ref[pl.ds((i * TAPS + lag) * blocks, blocks), :] for lag in range(TAPS)]


def features_kernel(stream_ref, taps_ref, after_ref, product_ref, edge_ref, wide_ref):
    rows = stream_ref.shape[1]
    blocks = stream_ref.shape[2] // LANES
    span = SUB * blocks
    last_pair = rows // (2 * SUB) - 1
    for i in range(3):
        spread_tokens(stream_ref.at[i], wide_ref.at[i], range(last_pair + 1) if i else (last_pair,))
    taps = [load_taps(taps_ref, blocks, i) for i in range(3)]

    def token(i, start, s):
        return wide_ref[i, pl.ds(start + s, blocks, stride=SUB), :]

    def step(b, carry):
        before = [list(c) for c in carry]
        start = pl.multiple_of(b * span, span)
        for s in range(SUB):
            feats = []
            for i in (1, 2):
                now = token(i, start, s)
                older, old = before[i - 1]
                feats.append(taps[i][0] * now + taps[i][1] * old + taps[i][2] * older)
                before[i - 1] = [old, now]
            product_ref[pl.ds(pl.multiple_of(b * span + s * blocks, blocks), blocks), :] = feats[0] * feats[1]
        return tuple(tuple(c) for c in before)

    zero = jnp.zeros((blocks, LANES), F32)
    lax.fori_loop(0, rows // SUB, step, ((zero, zero),) * 2)

    def put(row, value):
        edge_ref[pl.ds(row * blocks, blocks), :] = value

    for i in range(3):
        old, now = token(i, (rows - SUB) * blocks, SUB - 2), token(i, (rows - SUB) * blocks, SUB - 1)
        put(2 * i, taps[i][1] * now + taps[i][2] * old)
        put(2 * i + 1, taps[i][2] * now)
    for i in (1, 2):
        first, second = token(i, 0, 0), token(i, 0, 1)
        put(2 * i + 4, taps[i][0] * first)
        put(2 * i + 5, taps[i][0] * second + taps[i][1] * first)
    product_ref[pl.ds(0, blocks), :] = zero
    product_ref[pl.ds(blocks, blocks), :] = zero


def state_kernel(product_ref, poles_ref, edge_ref, state_ref, decay_ref, residue_ref, rate_ref, wide_ref):
    blocks = SUB
    rows = product_ref.shape[0] // blocks
    poles = poles_ref[...]
    lane = lax.broadcasted_iota(jnp.int32, (ORDER, LANES), 1)
    for j in range(blocks):
        group = lane // GROUP + j * (LANES // GROUP)
        wide_ref[0, pl.ds(j * ORDER, ORDER), :] = jnp.take_along_axis(poles, group, axis=1)
        wide_ref[1, pl.ds(j * ORDER, ORDER), :] = jnp.take_along_axis(poles, group + LANES // 2, axis=1)
    rates, decays = [], []
    for r in range(ORDER):
        rate = wide_ref[0, pl.ds(r, blocks, stride=ORDER), :]
        decay = jnp.exp(-rate)
        decay_ref[pl.ds(r * blocks, blocks), :] = decay
        residue_ref[pl.ds(r * blocks, blocks), :] = wide_ref[1, pl.ds(r, blocks, stride=ORDER), :]
        rates.append(rate)
        decays.append(decay)
    store_slices(rate_ref, rates, PART)
    for n in range(EDGES):
        parts = swap_halves(*[edge_ref[pl.ds((2 * n + t) * blocks, blocks), :] for t in range(2)])
        for c in range(CUTS):
            state_ref[pl.ds(SEND * c + PART + n, SUB, stride=CUTS * SEND), :] = parts[c]
    zero = jnp.zeros((blocks, LANES), F32)

    def step(b, states):
        states = list(states)
        for s in range(SUB):
            p = product_ref[pl.ds(pl.multiple_of((b * SUB + s) * blocks, blocks), blocks), :]
            states = [decays[r] * states[r] + p for r in range(ORDER)]
        return tuple(states)

    store_slices(state_ref, lax.fori_loop(0, rows // SUB, step, (zero,) * ORDER), SEND)


def local_kernel(product_ref, decay_ref, residue_ref, taps_ref, after_ref, stream, out_ref, query_ref, source_v, wide_ref, sem):
    blocks = SUB
    span = SUB * blocks
    rows = product_ref.shape[0] // blocks
    copy = pltpu.make_async_copy(stream.at[0], source_v, sem.at[0])
    copy.start()
    decays = [decay_ref[pl.ds(r * blocks, blocks), :] for r in range(ORDER)]
    residues = [residue_ref[pl.ds(r * blocks, blocks), :] for r in range(ORDER)]

    def step(b, states):
        states = list(states)
        for s in range(SUB):
            at = pl.ds(pl.multiple_of((b * SUB + s) * blocks, blocks), blocks)
            p = product_ref[at, :]
            states = [decays[r] * states[r] + p for r in range(ORDER)]
            out_ref[at, :] = total([residues[r] * states[r] for r in range(ORDER)])
        return tuple(states)

    zero = jnp.zeros((blocks, LANES), F32)
    lax.fori_loop(0, rows // SUB, step, (zero,) * ORDER)
    copy.wait()
    spread_tokens(source_v, wide_ref, range(rows // (2 * SUB)))
    taps = load_taps(taps_ref, blocks, 0)

    def filtered(b, before):
        older, old = before
        for s in range(SUB):
            now = wide_ref[pl.ds(pl.multiple_of(b * span, span) + s, blocks, stride=SUB), :]
            at = pl.ds(pl.multiple_of((b * SUB + s) * blocks, blocks), blocks)
            query_ref[at, :] = taps[0] * now + taps[1] * old + taps[2] * older
            older, old = old, now
        return older, old

    lax.fori_loop(0, rows // SUB, filtered, (zero, zero))


def total(terms):
    while len(terms) > 1:
        terms = [terms[k] + terms[k + 1] for k in range(0, len(terms), 2)]
    return terms[0]


def edge_state(own, previous, powers_ref):
    product = (own[3:4] + previous[1:2]) * (own[4:5] + previous[2:3])
    mask = low_half(product.shape)
    turned = half_turn(product)
    return powers_ref[0] * jnp.where(mask, product, turned) + powers_ref[1] * jnp.where(mask, turned, product)


def near_kernel(rows, parts_ref, rate_ref, message_ref, powers_ref, prefix_ref, halo_ref):
    count = parts_ref.shape[0] // SEND
    position = lax.axis_index("ctx")
    rate = rate_ref[lax.rem(position, count)]
    for n, length in enumerate((rows - 1, rows - 2, rows, rows * (count - 1), rows * count)):
        powers_ref[n] = jnp.exp(-rate * float(length))
    run = jnp.zeros(rate.shape, F32)
    none = jnp.zeros((3, LANES), F32)
    previous = none
    halo_ref[:3, :] = none
    for k in range(count):
        prefix_ref[k] = run
        new = parts_ref[pl.ds(SEND * k, PART), :]
        edges = parts_ref[pl.ds(SEND * k + PART, EDGES), :]
        if k:
            halo_ref[pl.ds(3 * k, 3), :] = previous
            new = new + edge_state(edges, previous, powers_ref)
        run = powers_ref[2] * run + new
        previous = edges[:3]
    first = parts_ref[pl.ds(PART, EDGES), :]
    start = run + powers_ref[3] * edge_state(first, none, powers_ref)
    message_ref[:PART, :] = jnp.where(position < count, start, run)
    message_ref[pl.ds(PART, 3), :] = previous
    message_ref[pl.ds(PART + 3, 2), :] = first[3:]


def link_kernel(z, count, message_ref, heard_ref, got_ref, powers_ref, message_out, heard_out):
    heard_out[...] = heard_ref[...] + got_ref[...]
    mine = message_ref[:PART, :]
    edges = message_ref[pl.ds(PART, EDGES), :]
    whole = powers_ref[4] * got_ref[:PART, :] + mine
    whole = whole + powers_ref[3] * edge_state(edges, got_ref[pl.ds(PART, EDGES), :], powers_ref)
    message_out[:PART, :] = jnp.where(lax.axis_index("ctx") // count == z + 1, whole, mine)
    message_out[pl.ds(PART, EDGES), :] = edges


def spread_kernel(message_ref, heard_ref, jumps_ref, powers_ref, prefix_ref, halo_ref, out_ref):
    count = prefix_ref.shape[0]
    index = lax.axis_index("ctx") // count
    run = heard_ref[:PART, :]
    halo = heard_ref[pl.ds(PART, EDGES), :]
    for n, far in enumerate(JUMPS):
        source = index - far
        value = jumps_ref[n][:PART, :]
        edges = jumps_ref[n][pl.ds(PART, EDGES), :]
        later = powers_ref[4] * run + value + powers_ref[3] * edge_state(edges, halo, powers_ref)
        run = jnp.where(source == CHAIN - 1, value, jnp.where(source >= CHAIN, later, run))
        halo = jnp.where(source >= CHAIN - 1, edges, halo)
    first = edge_state(message_ref[pl.ds(PART, EDGES), :], halo, powers_ref)
    for k in range(count):
        out_ref[pl.ds(BACK * k, PART), :] = prefix_ref[k] + run
        out_ref[pl.ds(BACK * k + PART, 3), :] = halo_ref[pl.ds(3 * k, 3), :] if k else halo[:3]
        run = powers_ref[2] * run
        if k == 0:
            run = run + first


def output_kernel(start_ref, product_ref, query_ref, edge_ref, local_ref, decay_ref, residue_ref, out, wide_ref, out_v, sems):
    blocks = SUB
    span = SUB * blocks
    rows = product_ref.shape[0] // blocks
    decays = [decay_ref[pl.ds(r * blocks, blocks), :] for r in range(ORDER)]
    residues = [residue_ref[pl.ds(r * blocks, blocks), :] for r in range(ORDER)]
    pairs = [load_pair(start_ref, a) for a in range(PART)]
    states = [low for low, _ in pairs] + [high for _, high in pairs]

    halos = [load_pair(start_ref, PART + n) for n in range(3)]
    carried = states
    for s in range(TAPS - 1):
        one, two = [edge_ref[pl.ds((2 * n + s) * blocks, blocks), :] + halos[n - 2][s] for n in (3, 4)]
        carried = [decays[r] * carried[r] + one * two for r in range(ORDER)]
        terms = [residues[r] * carried[r] for r in range(ORDER)]
        q = query_ref[pl.ds(s * blocks, blocks), :] + halos[0][s]
        wide_ref[pl.ds(s, blocks, stride=SUB), :] = q * total(terms)

    def token(b, s, terms):
        at = pl.ds(pl.multiple_of((b * SUB + s) * blocks, blocks), blocks)
        terms = [decays[r] * terms[r] for r in range(ORDER)]
        wide_ref[pl.ds(b * span + s, blocks, stride=SUB), :] = query_ref[at, :] * (local_ref[at, :] + total(terms))
        return terms

    def step(b, terms):
        terms = list(terms)
        for s in range(SUB):
            terms = token(b, s, terms)
        return tuple(terms)

    for s in range(TAPS - 1, SUB):
        terms = token(0, s, terms)
    size = rows // PIECES
    copies = []
    for piece in range(PIECES):
        first, end = piece * size // SUB, (piece + 1) * size // SUB
        terms = lax.fori_loop(max(first, 1), end, step, tuple(terms))
        for pair in range(first // 2, end // 2):
            for j in range(blocks):
                base = 2 * pair * span + j * SUB
                both = jnp.concatenate([wide_ref[pl.ds(base, SUB), :], wide_ref[pl.ds(base + span, SUB), :]], 0)
                out_v[pair * 2 * SUB : (pair + 1) * 2 * SUB, j * LANES : (j + 1) * LANES] = both.astype(out_v.dtype)
        part = pl.ds(piece * size, size)
        copies.append(pltpu.make_async_copy(out_v.at[part, :], out.at[part, :], sems.at[piece]))
        copies[-1].start()
    for copy in copies:
        copy.wait()


def shape(*dims):
    return pltpu.VMEM(dims, F32)


def call(kernel, out_shape, inputs, scratch=()):
    return pl.pallas_call(kernel, out_shape=out_shape, scratch_shapes=list(scratch))(
        *[pltpu.with_memory_space_constraint(x, pltpu.VMEM) for x in inputs]
    )


def exchange(x, groups):
    flat = x.reshape(len(groups[0]), 1, -1)
    flat = lax.all_to_all(flat, "ctx", split_axis=0, concat_axis=0, tiled=True, axis_index_groups=groups)
    return flat.reshape(x.shape)


def earlier_runs(message, powers, run):
    def send(value, routes):
        pairs = [(a * run + k, b * run + k) for a, b in routes for k in range(run)]
        return lax.ppermute(value, "ctx", pairs)

    heard = jnp.zeros((SEND, LANES), F32)
    row = shape(SEND, LANES)
    for z in range(CHAIN - 1):
        got = send(message, [(z, z + 1)])
        message, heard = call(functools.partial(link_kernel, z, run), (row, row), (message, heard, got, powers))
    jumps = [send(message, [(z, z + far) for z in range(CHAIN - 1, RUNS - far)]) for far in JUMPS]
    return message, heard, jumps


def block(stream, short_taps, decay_rate, residue):
    rows, chans = stream.shape[1], stream.shape[2]
    blocks = chans // LANES
    ctx_size, dp_size = lax.axis_size("ctx"), lax.axis_size("dp")

    packed, near_stream, taps = pl.pallas_call(
        pack_kernel,
        in_specs=[pl.BlockSpec(memory_space=pl.ANY)] * 4,
        out_shape=(
            shape(dp_size, decay_rate.shape[0], LANES),
            pltpu.VMEM(stream.shape, stream.dtype),
            shape(3 * TAPS * blocks, LANES),
        ),
        scratch_shapes=[
            pltpu.VMEM((3, TAPS, chans), F32),
            pltpu.VMEM(decay_rate.shape, F32),
            pltpu.VMEM(residue.shape, F32),
            pltpu.SemaphoreType.DMA((4,)),
        ],
        name="pack",
    )(stream, short_taps, decay_rate, residue)
    poles = lax.all_to_all(packed, "dp", split_axis=0, concat_axis=0, tiled=True)
    poles = poles.reshape(ORDER, LANES)

    token_major = shape(rows * blocks, LANES)
    product, edges = call(
        features_kernel,
        (token_major, shape(2 * EDGES * blocks, LANES)),
        (near_stream, taps, poles),
        (pltpu.VMEM((3, rows * blocks, LANES), F32),),
    )
    table = shape(ORDER * blocks, LANES)
    run = ctx_size // RUNS
    state, decay, gain, rate = call(
        state_kernel,
        (shape(run * SEND, LANES), table, table, table),
        (product, poles, edges),
        (pltpu.VMEM((2, ORDER * blocks, LANES), F32),),
    )

    near = [[z * run + k for k in range(run)] for z in range(RUNS)]
    parts = exchange(state, near)
    message, powers, prefix, halos = call(
        functools.partial(near_kernel, rows),
        (shape(SEND, LANES), shape(5, PART, LANES), shape(run, PART, LANES), shape(3 * run, LANES)),
        (parts, rate.reshape(run, PART, LANES)),
    )
    vmem = functools.partial(pltpu.with_memory_space_constraint, memory_space=pltpu.VMEM)
    local, query = pl.pallas_call(
        local_kernel,
        in_specs=[pl.BlockSpec(memory_space=pltpu.VMEM)] * 5 + [pl.BlockSpec(memory_space=pl.ANY)],
        out_shape=(token_major, token_major),
        scratch_shapes=[
            pltpu.VMEM((rows, chans), stream.dtype),
            pltpu.VMEM((rows * blocks, LANES), F32),
            pltpu.SemaphoreType.DMA((1,)),
        ],
        name="local",
    )(vmem(product), vmem(decay), vmem(gain), vmem(taps), vmem(message), stream)
    message, heard, jumps = earlier_runs(message, powers, run)

    def spread(message_ref, heard_ref, *refs):
        spread_kernel(message_ref, heard_ref, refs[: len(jumps)], *refs[len(jumps) :])

    starts = call(spread, shape(run * BACK, LANES), (message, heard, *jumps, powers, prefix, halos))
    inputs = (exchange(starts, near), product, query, edges, local, decay, gain)
    return pl.pallas_call(
        output_kernel,
        in_specs=[pl.BlockSpec(memory_space=pltpu.VMEM)] * len(inputs),
        out_specs=pl.BlockSpec(memory_space=pl.ANY),
        out_shape=jax.ShapeDtypeStruct((rows, chans), jnp.bfloat16),
        scratch_shapes=[
            pltpu.VMEM((rows * blocks, LANES), F32),
            pltpu.VMEM((rows, chans), jnp.bfloat16),
            pltpu.SemaphoreType.DMA((PIECES,)),
        ],
        name="output",
    )(*[vmem(x) for x in inputs])


def solution(mesh):
    in_specs = (P(None, "ctx", "dp"), P(), P("dp", None), P("dp", None))
    out_specs = P("ctx", "dp")
    return jax.shard_map(block, mesh=mesh, in_specs=in_specs, out_specs=out_specs, check_vma=False)
```

```python
import functools

import jax
import jax.numpy as jnp
from jax import lax
from jax.experimental import pallas as pl
from jax.experimental.pallas import tpu as pltpu
from jax.sharding import PartitionSpec as P


GROUP = 16
ORDER = 16
TAPS = 3
LANES = 128
SUB = 8
CUTS = 2
PART = ORDER // CUTS
EDGES = 5
SEND = PART + EDGES
BACK = PART + 3
RUNS = 8
CHAIN = 5
JUMPS = (2, 3, 1)
PIECES = 4
F32 = jnp.float32


def low_half(shape):
    return lax.broadcasted_iota(jnp.int32, shape, len(shape) - 1) < LANES // 2


def half_turn(x):
    return pltpu.roll(x, LANES // 2, x.ndim - 1)


def swap_halves(first, second):
    mask = low_half(first.shape)
    return jnp.where(mask, first, half_turn(second)), jnp.where(mask, half_turn(first), second)


def store_slices(ref, vectors, chunk):
    for a in range(PART):
        for c, vector in enumerate(swap_halves(vectors[a], vectors[a + PART])):
            ref[pl.ds(chunk * c + a, SUB, stride=CUTS * chunk), :] = vector


def load_pair(ref, row):
    return swap_halves(*[ref[pl.ds(BACK * c + row, SUB, stride=CUTS * BACK), :] for c in range(CUTS)])


def pack_kernel(stream, taps, rates, residues, out_ref, stream_ref, taps_ref, taps_v, rate_v, residue_v, sems):
    count, _, chans = taps_v.shape
    offset = pl.multiple_of(lax.axis_index("dp") * chans, LANES)
    copies = [
        pltpu.make_async_copy(rates, rate_v, sems.at[0]),
        pltpu.make_async_copy(residues, residue_v, sems.at[1]),
        pltpu.make_async_copy(taps.at[:, :, pl.ds(offset, chans)], taps_v, sems.at[2]),
        pltpu.make_async_copy(stream, stream_ref, sems.at[3]),
    ]
    for copy in copies:
        copy.start()
    copies[0].wait()
    copies[1].wait()
    mask = low_half((rate_v.shape[0], LANES))
    for q in range(rate_v.shape[1] // LANES):
        rate = rate_v[:, q * LANES : (q + 1) * LANES]
        residue = residue_v[:, q * LANES : (q + 1) * LANES]
        out_ref[2 * q] = jnp.where(mask, rate, half_turn(residue))
        out_ref[2 * q + 1] = jnp.where(mask, half_turn(rate), residue)
    copies[2].wait()
    blocks = chans // LANES
    for i in range(count):
        for lag in range(TAPS):
            for j in range(blocks):
                taps_ref[pl.ds((i * TAPS + lag) * blocks + j, 1), :] = taps_v[
                    i, pl.ds(lag, 1), j * LANES : (j + 1) * LANES
                ]
    copies[3].wait()


def spread_tokens(source_ref, wide_ref, pairs):
    blocks = source_ref.shape[1] // LANES
    span = SUB * blocks
    for pair in pairs:
        for j in range(blocks):
            both = source_ref[pair * 2 * SUB : (pair + 1) * 2 * SUB, j * LANES : (j + 1) * LANES].astype(F32)
            base = 2 * pair * span + j * SUB
            wide_ref[pl.ds(base, SUB), :] = both[:SUB]
            wide_ref[pl.ds(base + span, SUB), :] = both[SUB:]


def load_taps(taps_ref, blocks, i):
    return [taps_ref[pl.ds((i * TAPS + lag) * blocks, blocks), :] for lag in range(TAPS)]


def features_kernel(stream_ref, taps_ref, after_ref, product_ref, edge_ref, wide_ref):
    rows = stream_ref.shape[1]
    blocks = stream_ref.shape[2] // LANES
    span = SUB * blocks
    last_pair = rows // (2 * SUB) - 1
    for i in range(3):
        spread_tokens(stream_ref.at[i], wide_ref.at[i], range(last_pair + 1) if i else (last_pair,))
    taps = [load_taps(taps_ref, blocks, i) for i in range(3)]

    def token(i, start, s):
        return wide_ref[i, pl.ds(start + s, blocks, stride=SUB), :]

    def step(b, carry):
        before = [list(c) for c in carry]
        start = pl.multiple_of(b * span, span)
        for s in range(SUB):
            feats = []
            for i in (1, 2):
                now = token(i, start, s)
                older, old = before[i - 1]
                feats.append(taps[i][0] * now + taps[i][1] * old + taps[i][2] * older)
                before[i - 1] = [old, now]
            product_ref[pl.ds(pl.multiple_of(b * span + s * blocks, blocks), blocks), :] = feats[0] * feats[1]
        return tuple(tuple(c) for c in before)

    zero = jnp.zeros((blocks, LANES), F32)
    lax.fori_loop(0, rows // SUB, step, ((zero, zero),) * 2)

    def put(row, value):
        edge_ref[pl.ds(row * blocks, blocks), :] = value

    for i in range(3):
        old, now = token(i, (rows - SUB) * blocks, SUB - 2), token(i, (rows - SUB) * blocks, SUB - 1)
        put(2 * i, taps[i][1] * now + taps[i][2] * old)
        put(2 * i + 1, taps[i][2] * now)
    for i in (1, 2):
        first, second = token(i, 0, 0), token(i, 0, 1)
        put(2 * i + 4, taps[i][0] * first)
        put(2 * i + 5, taps[i][0] * second + taps[i][1] * first)
    product_ref[pl.ds(0, blocks), :] = zero
    product_ref[pl.ds(blocks, blocks), :] = zero


def state_kernel(product_ref, poles_ref, edge_ref, state_ref, decay_ref, residue_ref, rate_ref, wide_ref):
    blocks = SUB
    rows = product_ref.shape[0] // blocks
    poles = poles_ref[...]
    lane = lax.broadcasted_iota(jnp.int32, (ORDER, LANES), 1)
    for j in range(blocks):
        group = lane // GROUP + j * (LANES // GROUP)
        wide_ref[0, pl.ds(j * ORDER, ORDER), :] = jnp.take_along_axis(poles, group, axis=1)
        wide_ref[1, pl.ds(j * ORDER, ORDER), :] = jnp.take_along_axis(poles, group + LANES // 2, axis=1)
    rates, decays = [], []
    for r in range(ORDER):
        rate = wide_ref[0, pl.ds(r, blocks, stride=ORDER), :]
        decay = jnp.exp(-rate)
        decay_ref[pl.ds(r * blocks, blocks), :] = decay
        residue_ref[pl.ds(r * blocks, blocks), :] = wide_ref[1, pl.ds(r, blocks, stride=ORDER), :]
        rates.append(rate)
        decays.append(decay)
    store_slices(rate_ref, rates, PART)
    for n in range(EDGES):
        parts = swap_halves(*[edge_ref[pl.ds((2 * n + t) * blocks, blocks), :] for t in range(2)])
        for c in range(CUTS):
            state_ref[pl.ds(SEND * c + PART + n, SUB, stride=CUTS * SEND), :] = parts[c]
    zero = jnp.zeros((blocks, LANES), F32)

    def step(b, states):
        states = list(states)
        for s in range(SUB):
            p = product_ref[pl.ds(pl.multiple_of((b * SUB + s) * blocks, blocks), blocks), :]
            states = [decays[r] * states[r] + p for r in range(ORDER)]
        return tuple(states)

    store_slices(state_ref, lax.fori_loop(0, rows // SUB, step, (zero,) * ORDER), SEND)


def local_kernel(product_ref, decay_ref, residue_ref, taps_ref, after_ref, stream, out_ref, query_ref, source_v, wide_ref, sem):
    blocks = SUB
    span = SUB * blocks
    rows = product_ref.shape[0] // blocks
    copy = pltpu.make_async_copy(stream.at[0], source_v, sem.at[0])
    copy.start()
    decays = [decay_ref[pl.ds(r * blocks, blocks), :] for r in range(ORDER)]
    residues = [residue_ref[pl.ds(r * blocks, blocks), :] for r in range(ORDER)]

    def step(b, states):
        states = list(states)
        for s in range(SUB):
            at = pl.ds(pl.multiple_of((b * SUB + s) * blocks, blocks), blocks)
            p = product_ref[at, :]
            states = [decays[r] * states[r] + p for r in range(ORDER)]
            out_ref[at, :] = total([residues[r] * states[r] for r in range(ORDER)])
        return tuple(states)

    zero = jnp.zeros((blocks, LANES), F32)
    lax.fori_loop(0, rows // SUB, step, (zero,) * ORDER)
    copy.wait()
    spread_tokens(source_v, wide_ref, range(rows // (2 * SUB)))
    taps = load_taps(taps_ref, blocks, 0)

    def filtered(b, before):
        older, old = before
        for s in range(SUB):
            now = wide_ref[pl.ds(pl.multiple_of(b * span, span) + s, blocks, stride=SUB), :]
            at = pl.ds(pl.multiple_of((b * SUB + s) * blocks, blocks), blocks)
            query_ref[at, :] = taps[0] * now + taps[1] * old + taps[2] * older
            older, old = old, now
        return older, old

    lax.fori_loop(0, rows // SUB, filtered, (zero, zero))


def total(terms):
    while len(terms) > 1:
        terms = [terms[k] + terms[k + 1] for k in range(0, len(terms), 2)]
    return terms[0]


def edge_state(own, previous, powers_ref):
    product = (own[3:4] + previous[1:2]) * (own[4:5] + previous[2:3])
    mask = low_half(product.shape)
    turned = half_turn(product)
    return powers_ref[0] * jnp.where(mask, product, turned) + powers_ref[1] * jnp.where(mask, turned, product)


def near_kernel(rows, parts_ref, rate_ref, message_ref, powers_ref, prefix_ref, halo_ref):
    count = parts_ref.shape[0] // SEND
    position = lax.axis_index("ctx")
    rate = rate_ref[lax.rem(position, count)]
    for n, length in enumerate((rows - 1, rows - 2, rows, rows * (count - 1), rows * count)):
        powers_ref[n] = jnp.exp(-rate * float(length))
    run = jnp.zeros(rate.shape, F32)
    none = jnp.zeros((3, LANES), F32)
    previous = none
    halo_ref[:3, :] = none
    for k in range(count):
        prefix_ref[k] = run
        new = parts_ref[pl.ds(SEND * k, PART), :]
        edges = parts_ref[pl.ds(SEND * k + PART, EDGES), :]
        if k:
            halo_ref[pl.ds(3 * k, 3), :] = previous
            new = new + edge_state(edges, previous, powers_ref)
        run = powers_ref[2] * run + new
        previous = edges[:3]
    first = parts_ref[pl.ds(PART, EDGES), :]
    start = run + powers_ref[3] * edge_state(first, none, powers_ref)
    message_ref[:PART, :] = jnp.where(position < count, start, run)
    message_ref[pl.ds(PART, 3), :] = previous
    message_ref[pl.ds(PART + 3, 2), :] = first[3:]


def link_kernel(z, count, message_ref, heard_ref, got_ref, powers_ref, message_out, heard_out):
    heard_out[...] = heard_ref[...] + got_ref[...]
    mine = message_ref[:PART, :]
    edges = message_ref[pl.ds(PART, EDGES), :]
    whole = powers_ref[4] * got_ref[:PART, :] + mine
    whole = whole + powers_ref[3] * edge_state(edges, got_ref[pl.ds(PART, EDGES), :], powers_ref)
    message_out[:PART, :] = jnp.where(lax.axis_index("ctx") // count == z + 1, whole, mine)
    message_out[pl.ds(PART, EDGES), :] = edges


def spread_kernel(message_ref, heard_ref, jumps_ref, powers_ref, prefix_ref, halo_ref, out_ref):
    count = prefix_ref.shape[0]
    index = lax.axis_index("ctx") // count
    run = heard_ref[:PART, :]
    halo = heard_ref[pl.ds(PART, EDGES), :]
    for n, far in enumerate(sorted(JUMPS, reverse=True)):
        source = index - far
        value = jumps_ref[n][:PART, :]
        edges = jumps_ref[n][pl.ds(PART, EDGES), :]
        later = powers_ref[4] * run + value + powers_ref[3] * edge_state(edges, halo, powers_ref)
        run = jnp.where(source == CHAIN - 1, value, jnp.where(source >= CHAIN, later, run))
        halo = jnp.where(source >= CHAIN - 1, edges, halo)
    first = edge_state(message_ref[pl.ds(PART, EDGES), :], halo, powers_ref)
    for k in range(count):
        out_ref[pl.ds(BACK * k, PART), :] = prefix_ref[k] + run
        out_ref[pl.ds(BACK * k + PART, 3), :] = halo_ref[pl.ds(3 * k, 3), :] if k else halo[:3]
        run = powers_ref[2] * run
        if k == 0:
            run = run + first


def output_kernel(start_ref, product_ref, query_ref, edge_ref, local_ref, decay_ref, residue_ref, out, wide_ref, out_v, sems):
    blocks = SUB
    span = SUB * blocks
    rows = product_ref.shape[0] // blocks
    decays = [decay_ref[pl.ds(r * blocks, blocks), :] for r in range(ORDER)]
    residues = [residue_ref[pl.ds(r * blocks, blocks), :] for r in range(ORDER)]
    pairs = [load_pair(start_ref, a) for a in range(PART)]
    states = [low for low, _ in pairs] + [high for _, high in pairs]

    halos = [load_pair(start_ref, PART + n) for n in range(3)]
    carried = states
    for s in range(TAPS - 1):
        one, two = [edge_ref[pl.ds((2 * n + s) * blocks, blocks), :] + halos[n - 2][s] for n in (3, 4)]
        carried = [decays[r] * carried[r] + one * two for r in range(ORDER)]
        terms = [residues[r] * carried[r] for r in range(ORDER)]
        q = query_ref[pl.ds(s * blocks, blocks), :] + halos[0][s]
        wide_ref[pl.ds(s, blocks, stride=SUB), :] = q * total(terms)

    def token(b, s, terms):
        at = pl.ds(pl.multiple_of((b * SUB + s) * blocks, blocks), blocks)
        terms = [decays[r] * terms[r] for r in range(ORDER)]
        wide_ref[pl.ds(b * span + s, blocks, stride=SUB), :] = query_ref[at, :] * (local_ref[at, :] + total(terms))
        return terms

    def step(b, terms):
        terms = list(terms)
        for s in range(SUB):
            terms = token(b, s, terms)
        return tuple(terms)

    for s in range(TAPS - 1, SUB):
        terms = token(0, s, terms)
    size = rows // PIECES
    copies = []
    for piece in range(PIECES):
        first, end = piece * size // SUB, (piece + 1) * size // SUB
        terms = lax.fori_loop(max(first, 1), end, step, tuple(terms))
        for pair in range(first // 2, end // 2):
            for j in range(blocks):
                base = 2 * pair * span + j * SUB
                both = jnp.concatenate([wide_ref[pl.ds(base, SUB), :], wide_ref[pl.ds(base + span, SUB), :]], 0)
                out_v[pair * 2 * SUB : (pair + 1) * 2 * SUB, j * LANES : (j + 1) * LANES] = both.astype(out_v.dtype)
        part = pl.ds(piece * size, size)
        copies.append(pltpu.make_async_copy(out_v.at[part, :], out.at[part, :], sems.at[piece]))
        copies[-1].start()
    for copy in copies:
        copy.wait()


def shape(*dims):
    return pltpu.VMEM(dims, F32)


def call(kernel, out_shape, inputs, scratch=()):
    return pl.pallas_call(kernel, out_shape=out_shape, scratch_shapes=list(scratch))(
        *[pltpu.with_memory_space_constraint(x, pltpu.VMEM) for x in inputs]
    )


def exchange(x, groups):
    flat = x.reshape(len(groups[0]), 1, -1)
    flat = lax.all_to_all(flat, "ctx", split_axis=0, concat_axis=0, tiled=True, axis_index_groups=groups)
    return flat.reshape(x.shape)


def earlier_runs(message, powers, run):
    def send(value, routes):
        pairs = [(a * run + k, b * run + k) for a, b in routes for k in range(run)]
        return lax.ppermute(value, "ctx", pairs)

    heard = jnp.zeros((SEND, LANES), F32)
    row = shape(SEND, LANES)
    for z in range(CHAIN - 1):
        got = send(message, [(z, z + 1)])
        message, heard = call(functools.partial(link_kernel, z, run), (row, row), (message, heard, got, powers))
    got = {far: send(message, [(z, z + far) for z in range(CHAIN - 1, RUNS - far)]) for far in JUMPS}
    jumps = [got[far] for far in sorted(JUMPS, reverse=True)]
    return message, heard, jumps


def block(stream, short_taps, decay_rate, residue):
    rows, chans = stream.shape[1], stream.shape[2]
    blocks = chans // LANES
    ctx_size, dp_size = lax.axis_size("ctx"), lax.axis_size("dp")

    packed, near_stream, taps = pl.pallas_call(
        pack_kernel,
        in_specs=[pl.BlockSpec(memory_space=pl.ANY)] * 4,
        out_shape=(
            shape(dp_size, decay_rate.shape[0], LANES),
            pltpu.VMEM(stream.shape, stream.dtype),
            shape(3 * TAPS * blocks, LANES),
        ),
        scratch_shapes=[
            pltpu.VMEM((3, TAPS, chans), F32),
            pltpu.VMEM(decay_rate.shape, F32),
            pltpu.VMEM(residue.shape, F32),
            pltpu.SemaphoreType.DMA((4,)),
        ],
        name="pack",
    )(stream, short_taps, decay_rate, residue)
    poles = lax.all_to_all(packed, "dp", split_axis=0, concat_axis=0, tiled=True)
    poles = poles.reshape(ORDER, LANES)

    token_major = shape(rows * blocks, LANES)
    product, edges = call(
        features_kernel,
        (token_major, shape(2 * EDGES * blocks, LANES)),
        (near_stream, taps, poles),
        (pltpu.VMEM((3, rows * blocks, LANES), F32),),
    )
    table = shape(ORDER * blocks, LANES)
    run = ctx_size // RUNS
    state, decay, gain, rate = call(
        state_kernel,
        (shape(run * SEND, LANES), table, table, table),
        (product, poles, edges),
        (pltpu.VMEM((2, ORDER * blocks, LANES), F32),),
    )

    near = [[z * run + k for k in range(run)] for z in range(RUNS)]
    parts = exchange(state, near)
    message, powers, prefix, halos = call(
        functools.partial(near_kernel, rows),
        (shape(SEND, LANES), shape(5, PART, LANES), shape(run, PART, LANES), shape(3 * run, LANES)),
        (parts, rate.reshape(run, PART, LANES)),
    )
    vmem = functools.partial(pltpu.with_memory_space_constraint, memory_space=pltpu.VMEM)
    local, query = pl.pallas_call(
        local_kernel,
        in_specs=[pl.BlockSpec(memory_space=pltpu.VMEM)] * 5 + [pl.BlockSpec(memory_space=pl.ANY)],
        out_shape=(token_major, token_major),
        scratch_shapes=[
            pltpu.VMEM((rows, chans), stream.dtype),
            pltpu.VMEM((rows * blocks, LANES), F32),
            pltpu.SemaphoreType.DMA((1,)),
        ],
        name="local",
    )(vmem(product), vmem(decay), vmem(gain), vmem(taps), vmem(message), stream)
    message, heard, jumps = earlier_runs(message, powers, run)

    def spread(message_ref, heard_ref, *refs):
        spread_kernel(message_ref, heard_ref, refs[: len(jumps)], *refs[len(jumps) :])

    starts = call(spread, shape(run * BACK, LANES), (message, heard, *jumps, powers, prefix, halos))
    inputs = (exchange(starts, near), product, query, edges, local, decay, gain)
    return pl.pallas_call(
        output_kernel,
        in_specs=[pl.BlockSpec(memory_space=pltpu.VMEM)] * len(inputs),
        out_specs=pl.BlockSpec(memory_space=pl.ANY),
        out_shape=jax.ShapeDtypeStruct((rows, chans), jnp.bfloat16),
        scratch_shapes=[
            pltpu.VMEM((rows * blocks, LANES), F32),
            pltpu.VMEM((rows, chans), jnp.bfloat16),
            pltpu.SemaphoreType.DMA((PIECES,)),
        ],
        name="output",
    )(*[vmem(x) for x in inputs])


def solution(mesh):
    in_specs = (P(None, "ctx", "dp"), P(), P("dp", None), P("dp", None))
    out_specs = P("ctx", "dp")
    return jax.shard_map(block, mesh=mesh, in_specs=in_specs, out_specs=out_specs, check_vma=False)
```
